32 devices in a mesh: grp: 2 (over x), head: 16 (over z, y, core).
Axes of the slice: x: 2, y: 2, z: 4, core: 2. Of those that a mesh axis runs over, the one named last changes fastest.
Arguments:
- queries: bfloat16 [2048, 2, 16, 256], P('head', 'grp'), parts along dimension 1, may hold values from -12 to 12
- new_kv: bfloat16 [2048, 2, 2, 512], P('head', 'grp'), parts along dimension 1, may hold values from -4 to 4
- cache: bfloat16 [32, 256, 512], P(('grp', 'head')), parts along dimension 0, may hold values from -12 to 12
- resid: bfloat16 [2048, 2, 2048], P('head', 'grp'), parts along dimension 1, may hold values from -6 to 6
- w_out: bfloat16 [16, 256, 2048], P(None, 'head'), may hold values from -0.375 to 0.375
- norm_gain: float32 [2048], replicated, may hold values from 0.1 to 1.9
- expert_ids: int32 [2048, 2, 2], P('head', 'grp'), parts along dimension 1, may hold values from 0 to 15, all different within a row; in each aligned block of 128 rows (0 to 127, 128 to 255, ..., all dimensions but the last counted through in order) at most 32 rows name the same one
- expert_gates: float32 [2048, 2, 2], P('head', 'grp'), parts along dimension 1, may hold values from 0.2 to 1
- w_in: bfloat16 [16, 2048, 1024], P('head'), may hold values from -0.125 to 0.125
- w_down: bfloat16 [16, 512, 2048], P('head'), may hold values from -0.25 to 0.25
Outputs:
- layer_out: bfloat16 [2048, 2, 2048], P('head', 'grp'), parts along dimension 1
The draws below stay inside these ranges and needn't reach their ends.
There are 2 independent parts, one for each index of `grp`. The reference program is written for one: setup_inputs(seed, part) draws one part's arguments, and reference() takes and returns one part's arrays. A program takes and returns all parts, laid end to end along the dimension named above; an argument that names none is the same for every part. Nothing has to cross between parts.
Inputs may be any that keep to these rules, and one draw needn't show every extreme that they name: `expert_ids`: rows are taken in order over positions and then sequences; in each aligned block of 128 such rows (the rows of one device) no expert is named by more than 32 rows, a bound that some block reaches. A row names 2 different experts.
All inputs are finite; a program needn't handle non-finite values.
Results may differ from the reference program's by a relative error of at most 0.009.
Values may be sent and summed in bfloat16 or wider, within the bound.
A program may use at most 128 MiB of HBM per device.

```python
import math
import jax
import jax.numpy as jnp
import numpy as np
from jax import lax

D = 2048
HEADS = 16
KV_HEADS = 2
HD = 256
FF_E = 512
TOP = 2
SPAN = 2048
CACHE = 2048
SEQS = 1
ROWS = 128
EXPERTS = 16
CAP = 32
N_HEAD = 16


def draw_queries(key, part):
    full_shape = (SPAN, SEQS, HEADS, HD)
    values = 2.0 * jnp.clip(jax.random.normal(jax.random.fold_in(key, 1), full_shape, jnp.float32), -4.0, 4.0)
    return values.astype(jnp.bfloat16)


def draw_cache(key, part):
    full_shape = (SEQS * KV_HEADS, CACHE, 2 * HD)
    values = jnp.clip(jax.random.normal(jax.random.fold_in(key, 2), full_shape, jnp.float32), -4.0, 4.0)
    paged = values.reshape(SEQS * HEADS, CACHE // (HEADS // KV_HEADS), 2 * HD)
    return paged.astype(jnp.bfloat16)


def level_of(own_key, extent, pieces, least, high):
    loudness, own = 1.0, jax.random.fold_in(own_key, 6)
    for dim, blocks in pieces:
        steps = jnp.exp(jax.random.uniform(jax.random.fold_in(own, dim), (blocks,), jnp.float32, least / len(pieces), high / len(pieces)))
        loudness = loudness * jnp.repeat(steps, extent[dim] // blocks).reshape([-1 if axis == dim else 1 for axis in range(len(extent))])
    return loudness


def routed_block(own_key, own, number, rows, number_of, top, bound, skew):
    order = jax.random.permutation(own_key, number_of)
    packed, ordinary = shares(number_of, rows * top, bound, skew, True), shares(number_of, rows * top, bound, skew, False)
    places = jnp.arange(number_of)

    def named(lengths, rotation):
        used = int((lengths > 0).sum())
        fixed = max(1, used // 4)
        passed = fixed + (places - fixed + rotation * (used - fixed)) % max(1, number_of - fixed)
        return jnp.zeros((number_of,), jnp.int32).at[order[jnp.where(places < fixed, places, passed)]].set(jnp.asarray(lengths, jnp.int32))

    lengths = jnp.where(number % 4 == 0, named(packed, number // 4), named(ordinary, number - number // 4 - 1))
    mixed = jax.random.permutation(jax.random.fold_in(own, 3), number_of)
    source_of, taker = mixed[0:number_of // 2 * 2:2], mixed[1:number_of // 2 * 2:2]
    slack = jnp.minimum(lengths[source_of] - 1, bound - lengths[taker]) // 2
    slack = jnp.where((source_of == order[0]) | (taker == order[0]) | (lengths[taker] == 0), 0, jnp.maximum(slack, 0))
    passed = jax.random.randint(jax.random.fold_in(own, 4), (number_of // 2,), 0, 1 << 20) % (slack + 1)
    lengths = lengths.at[source_of].add(-passed).at[taker].add(passed)
    members = jnp.searchsorted(jnp.cumsum(lengths), jnp.arange(rows * top), side="right").astype(jnp.int32)
    table = members.reshape(top, rows).T
    table = table[jax.random.permutation(jax.random.fold_in(own, 1), rows)]
    rotation = jax.random.randint(jax.random.fold_in(own, 2), (rows, 1), 0, top)
    return jnp.take_along_axis(table, (jnp.arange(top)[None, :] + rotation) % top, axis=1)


def shares(amount, total, reach, slope, full):
    weights = [(1 << 20) // math.isqrt(rank ** slope) + 1 for rank in range(1, amount + 1)]
    largest = reach if full else min(reach, max(-(-total // amount), total * weights[0] // sum(weights)))
    least = 1 if total - largest >= amount - 1 else 0
    counts, rest = [largest] + [least] * (amount - 1), total - largest - least * (amount - 1)
    while rest > 0:
        free = [i for i in range(1, amount) if counts[i] < largest] or [i for i in range(1, amount) if counts[i] < reach]
        pool, remaining = sum([weights[i] for i in free]), rest
        for i in free:
            extra = min(reach - counts[i], max(1, remaining * weights[i] // pool), rest)
            counts[i] = counts[i] + extra
            rest = rest - extra
    return np.array(counts)


def noise(stream_key, shape, deviation, reach, shards=(), kind=jnp.bfloat16):
    result = deviation * jax.random.normal(stream_key, shape, jnp.float32)
    if shards:
        result = result * level_of(stream_key, shape, shards, -0.22, 0.18)
    return jnp.clip(result, -reach, reach).astype(kind)


def setup_inputs(seed: int = 0, part: int = 0) -> dict:
    streams_of = jax.random.split(jax.random.key(seed), 11)
    own_keys = jax.random.split(jax.random.fold_in(streams_of[10], part), 11)
    queries = draw_queries(jax.random.fold_in(jax.random.fold_in(streams_of[10], part), 71), part)
    new_kv = noise(own_keys[1], (SPAN, SEQS, KV_HEADS, 2 * HD), 1.0, 4.0, ((0, 16),))
    cache = draw_cache(jax.random.fold_in(jax.random.fold_in(streams_of[10], part), 71), part)
    resid = noise(own_keys[3], (SPAN, SEQS, D), 1.0, 6.0, ((0, 16),))
    w_out = noise(streams_of[4], (HEADS, HD, D), HD ** -0.5, 0.375, ((1, 16),))
    norm_gain = jnp.clip(1.0 + 0.18 * jax.random.normal(streams_of[5], (D,), jnp.float32), 0.1, 1.9)
    expert_ids_keys = jax.random.split(jax.random.fold_in(own_keys[6], 1), SPAN * SEQS // ROWS)
    expert_ids_turns = jax.random.permutation(jax.random.fold_in(own_keys[6], 3), SPAN * SEQS // ROWS)
    expert_ids = jax.vmap(lambda own, number: routed_block(jax.random.fold_in(own_keys[6], 2), own, number, ROWS, EXPERTS, TOP, CAP, 0))(expert_ids_keys, expert_ids_turns).reshape((SPAN, SEQS, TOP))
    expert_gates = jnp.clip(0.2 + 0.8 * jax.random.uniform(own_keys[7], (SPAN, SEQS, TOP), jnp.float32) ** level_of(own_keys[7], (SPAN, SEQS, TOP), ((0, 16),), -0.2, 0.2), 0.2, 1.0)
    w_in = noise(streams_of[8], (EXPERTS, D, 2 * FF_E), D ** -0.5, 0.125, ((0, 16),))
    w_down = noise(streams_of[9], (EXPERTS, FF_E, D), FF_E ** -0.5, 0.25, ((0, 16),))
    return dict(queries=queries, new_kv=new_kv, cache=cache, resid=resid, w_out=w_out, norm_gain=norm_gain, expert_ids=expert_ids, expert_gates=expert_gates, w_in=w_in, w_down=w_down)


def attend_slot(query_rows_all, new_keys, new_values, cached):
    length = query_rows_all.shape[0]
    block_rows = min(512, length)
    score_scale = HD ** (-0.5)
    old_keys = cached[:, :HD]
    old_values = cached[:, HD:]
    key_positions = jnp.arange(length, dtype=jnp.int32)

    def one_block(first_row):
        query_rows = lax.dynamic_slice_in_dim(query_rows_all, first_row, block_rows, 0)
        old_scores = jnp.dot(query_rows, old_keys.T, preferred_element_type=jnp.float32) * score_scale
        new_scores = jnp.dot(query_rows, new_keys.T, preferred_element_type=jnp.float32) * score_scale
        row_positions = first_row + jnp.arange(block_rows, dtype=jnp.int32)
        allowed = key_positions[None, :] <= row_positions[:, None]
        new_scores = jnp.where(allowed, new_scores, -jnp.inf)
        row_max = jnp.maximum(lax.optimization_barrier(jnp.max(old_scores, 1)), lax.optimization_barrier(jnp.max(new_scores, 1)))[:, None]
        old_exp = jnp.exp(old_scores - row_max)
        new_exp = jnp.exp(new_scores - row_max)
        denominator = lax.optimization_barrier(jnp.sum(old_exp, 1)) + lax.optimization_barrier(jnp.sum(new_exp, 1))
        weighted_sum = jnp.dot(old_exp.astype(jnp.bfloat16), old_values, preferred_element_type=jnp.float32)
        weighted_sum = weighted_sum + jnp.dot(new_exp.astype(jnp.bfloat16), new_values, preferred_element_type=jnp.float32)
        return (weighted_sum / denominator[:, None]).astype(jnp.bfloat16)
    starts = (jnp.arange(length // block_rows) * block_rows).astype(jnp.int32)
    return lax.map(one_block, starts).reshape(length, HD)

def reference(queries, new_kv, cache, resid, w_out, norm_gain, expert_ids, expert_gates, w_in, w_down):
    group_size = HEADS // KV_HEADS
    slot_count = SEQS * HEADS
    query_slots = queries.reshape(SPAN, slot_count, HD).transpose(1, 0, 2)
    pair_slots = new_kv.reshape(SPAN, SEQS * KV_HEADS, 2 * HD).transpose(1, 0, 2)
    cached_slots = cache.reshape(SEQS * KV_HEADS, CACHE, 2 * HD)

    def per_slot(slot_index):
        pair_index = (slot_index // group_size).astype(jnp.int32)
        slot_queries = lax.dynamic_index_in_dim(query_slots, slot_index, 0, keepdims=False)
        slot_pairs = lax.dynamic_index_in_dim(pair_slots, pair_index, 0, keepdims=False)
        slot_cache = lax.dynamic_index_in_dim(cached_slots, pair_index, 0, keepdims=False)
        return attend_slot(slot_queries, slot_pairs[:, :HD], slot_pairs[:, HD:], slot_cache)
    outputs = lax.map(per_slot, jnp.arange(slot_count, dtype=jnp.int32))
    attended = outputs.transpose(1, 0, 2).reshape(SPAN * SEQS, HEADS * HD)
    stream = resid.reshape(SPAN * SEQS, D).astype(jnp.float32)
    stream = stream + jnp.dot(attended, w_out.reshape(HEADS * HD, D), preferred_element_type=jnp.float32)
    normed = stream * lax.rsqrt(lax.optimization_barrier(jnp.mean(stream * stream, 1, keepdims=True)) + 1e-06) * norm_gain
    normed = normed.astype(jnp.bfloat16)
    flat_ids = expert_ids.reshape(-1).astype(jnp.int32)
    assignments = flat_ids.shape[0]
    onehot = (flat_ids[:, None] == jnp.arange(EXPERTS, dtype=jnp.int32)[None, :]).astype(jnp.int32)
    earlier = jnp.cumsum(onehot, 0).astype(jnp.int32) - onehot
    slot_rank = lax.optimization_barrier(jnp.sum(earlier * onehot, 1)).astype(jnp.int32)
    limit = N_HEAD * CAP
    target = (flat_ids * limit + slot_rank).astype(jnp.int32)
    table = jnp.full((EXPERTS * limit,), assignments, jnp.int32)
    table = table.at[target].set(jnp.arange(assignments).astype(jnp.int32))
    repeated = jnp.concatenate([jnp.repeat(normed, TOP, axis=0), jnp.zeros((1, D), jnp.bfloat16)], 0)

    def per_expert(inputs):
        row_index, gate_up, down_weight = inputs
        expert_rows = repeated[row_index]
        inner_act = jnp.dot(expert_rows, gate_up, preferred_element_type=jnp.float32)
        hidden = (jax.nn.silu(inner_act[:, :FF_E]) * inner_act[:, FF_E:]).astype(jnp.bfloat16)
        return jnp.dot(hidden, down_weight, preferred_element_type=jnp.float32).astype(jnp.bfloat16)
    results = lax.map(per_expert, (table.reshape(EXPERTS, limit), w_in, w_down))
    picked = results.reshape(EXPERTS * limit, D)[target].astype(jnp.float32)
    weighted = picked * expert_gates.reshape(-1)[:, None]
    expert_sum = weighted.reshape(SPAN * SEQS, TOP, D).sum(1)
    return (stream + expert_sum).astype(jnp.bfloat16).reshape(SPAN, SEQS, D)
```

```python
import functools

import jax
import jax.numpy as jnp
from jax import lax
from jax.experimental import pallas as pl
from jax.sharding import PartitionSpec as P

eps_norm = 1e-06


def attend_kernel(query_ref, cache_ref, new_ref, out_ref, *, block, old_block):
    head_width = query_ref.shape[1]
    step = pl.program_id(0)
    query_rows = query_ref[...] * jnp.asarray(head_width ** (-0.5), query_ref.dtype)

    def fold(carry, keys, values, mask):
        top, total, weighted = carry
        scores = lax.dot_general(
            query_rows, keys, (((1,), (1,)), ((), ())), preferred_element_type=jnp.float32
        )
        if mask is not None:
            scores = jnp.where(mask, scores, -jnp.inf)
        new_top = jnp.maximum(top, jnp.max(scores, 1, keepdims=True))
        exps = jnp.exp(scores - new_top)
        shrink = jnp.exp(top - new_top)
        total = total * shrink + jnp.sum(exps, 1, keepdims=True)
        weighted = weighted * shrink + jnp.dot(
            exps.astype(jnp.bfloat16), values, preferred_element_type=jnp.float32
        )
        return new_top, total, weighted

    rows = query_rows.shape[0]
    carry = (
        jnp.full((rows, 1), -jnp.inf, jnp.float32),
        jnp.zeros((rows, 1), jnp.float32),
        jnp.zeros((rows, head_width), jnp.float32),
    )
    row_at = lax.broadcasted_iota(jnp.int32, (rows, block), 0)
    col_at = lax.broadcasted_iota(jnp.int32, (rows, block), 1)
    here = pl.ds(step * block, block)
    carry = fold(
        carry, new_ref[here, :head_width], new_ref[here, head_width:], col_at <= row_at
    )
    for first in range(0, cache_ref.shape[0], old_block):
        part = pl.ds(first, old_block)
        carry = fold(carry, cache_ref[part, :head_width], cache_ref[part, head_width:], None)

    def earlier(index, carry):
        part = pl.ds(index * block, block)
        return fold(carry, new_ref[part, :head_width], new_ref[part, head_width:], None)

    top, total, weighted = lax.fori_loop(0, step, earlier, carry)
    out_ref[...] = (weighted / total).astype(out_ref.dtype)


def attend(queries, new_pairs, cached):
    length, head_width = queries.shape
    block = min(512, length)
    old_block = min(1024, cached.shape[0])
    return pl.pallas_call(
        functools.partial(attend_kernel, block=block, old_block=old_block),
        grid=(length // block,),
        in_specs=[
            pl.BlockSpec((block, head_width), lambda i: (i, 0)),
            pl.BlockSpec(cached.shape, lambda i: (0, 0)),
            pl.BlockSpec(new_pairs.shape, lambda i: (0, 0)),
        ],
        out_specs=pl.BlockSpec((block, head_width), lambda i: (i, 0)),
        out_shape=jax.ShapeDtypeStruct((length, head_width), jnp.bfloat16),
        cost_estimate=pl.CostEstimate(
            flops=4 * length * head_width * (length // 2 + cached.shape[0]),
            bytes_accessed=8 * length * head_width * 2,
            transcendentals=length * (length // 2 + cached.shape[0]),
        ),
    )(queries, cached, new_pairs)


def local(queries, new_kv, cache, resid, w_out, norm_gain, expert_ids, expert_gates, w_in, w_down):
    axis_count = lax.axis_size("head")
    local_rows = queries.shape[0]
    seq_count = queries.shape[1]
    head_count = queries.shape[2]
    head_width = queries.shape[3]
    pair_heads = new_kv.shape[2]
    group_size = head_count // pair_heads
    model_width = resid.shape[2]
    row_count = local_rows * seq_count
    slots = seq_count * pair_heads
    across = [[c * group_size + j for c in range(slots)] for j in range(group_size)]
    inside = [[c * group_size + j for j in range(group_size)] for c in range(slots)]
    query_slots = queries.reshape(local_rows, axis_count, head_width).transpose(1, 0, 2)
    pair_slots = new_kv.reshape(local_rows, slots, 2 * head_width).transpose(1, 0, 2)
    pair_slots = lax.all_to_all(
        pair_slots, "head", split_axis=0, concat_axis=0, axis_index_groups=across, tiled=True
    )
    cache_rows = lax.all_gather(cache[0], "head", axis=0, axis_index_groups=inside, tiled=True)
    pairs = lax.all_gather(pair_slots, "head", axis=0, axis_index_groups=inside, tiled=False)
    pairs = pairs.transpose(1, 0, 2, 3).reshape(axis_count * local_rows, 2 * head_width)
    head_queries = lax.all_to_all(query_slots, "head", split_axis=0, concat_axis=0, tiled=True)
    attended = attend(head_queries.reshape(-1, head_width), pairs, cache_rows)
    returned = lax.all_to_all(
        attended.reshape(axis_count, local_rows, head_width),
        "head",
        split_axis=0,
        concat_axis=0,
        tiled=True,
    )
    attn_rows = returned.reshape(seq_count, head_count, local_rows, head_width)
    attn_rows = attn_rows.transpose(2, 0, 1, 3).reshape(row_count, head_count * head_width)
    w_full = lax.all_gather(w_out, "head", axis=1, tiled=True)
    projected = jnp.dot(
        attn_rows,
        w_full.reshape(head_count * head_width, model_width),
        preferred_element_type=jnp.float32,
    )
    stream = resid.reshape(row_count, model_width).astype(jnp.float32) + projected
    normed = stream * lax.rsqrt(jnp.mean(stream * stream, 1, keepdims=True) + eps_norm) * norm_gain
    normed = normed.astype(jnp.bfloat16)
    top_count = expert_ids.shape[2]
    flat_ids = expert_ids.reshape(-1)
    local_experts = w_in.shape[0]
    experts = local_experts * axis_count
    capacity = max(2, 2 * row_count * top_count // experts)
    onehot = (flat_ids[:, None] == jnp.arange(experts, dtype=jnp.int32)[None, :]).astype(jnp.int32)
    earlier = jnp.cumsum(onehot, 0) - onehot
    slot_rank = jnp.sum(earlier * onehot, 1)
    target = flat_ids * capacity + slot_rank
    repeated = jnp.repeat(normed, top_count, axis=0)
    outgoing = jnp.zeros((experts * capacity, model_width), jnp.bfloat16).at[target].set(repeated)
    outgoing = outgoing.reshape(experts, 1, capacity, model_width)
    hidden_width = w_down.shape[1]
    inner_act = jnp.einsum(
        "esmd,edf->esmf",
        lax.all_to_all(outgoing, "head", split_axis=0, concat_axis=1, tiled=True),
        w_in,
        preferred_element_type=jnp.float32,
    )
    hidden = (jax.nn.silu(inner_act[..., :hidden_width]) * inner_act[..., hidden_width:]).astype(
        jnp.bfloat16
    )
    answered = jnp.einsum(
        "esmf,efd->esmd", hidden, w_down, preferred_element_type=jnp.float32
    ).astype(jnp.bfloat16)
    returned_rows = lax.all_to_all(answered, "head", split_axis=1, concat_axis=0, tiled=True)
    picked = returned_rows.reshape(experts * capacity, model_width)[target].astype(jnp.float32)
    weighted = picked * expert_gates.reshape(-1)[:, None]
    expert_sum = weighted.reshape(row_count, top_count, model_width).sum(1)
    return (stream + expert_sum).astype(jnp.bfloat16).reshape(local_rows, seq_count, model_width)


def solution(mesh):
    return jax.shard_map(
        local,
        mesh=mesh,
        in_specs=(
            P("head", "grp", None, None),
            P("head", "grp", None, None),
            P(("grp", "head"), None, None),
            P("head", "grp", None),
            P(None, "head", None),
            P(),
            P("head", "grp", None),
            P("head", "grp", None),
            P("head", None, None),
            P("head", None, None),
        ),
        out_specs=P("head", "grp", None),
        check_vma=False,
    )
```

```python
import functools

import jax
import jax.numpy as jnp
from jax import lax
from jax.experimental import pallas as pl
from jax.sharding import PartitionSpec as P

eps_norm = 1e-06


def swap_in_pair(value):
    pairs = [(source, source ^ 1) for source in range(lax.axis_size("head"))]
    return lax.ppermute(value, "head", pairs)


def attend_kernel(query_ref, cache_ref, other_ref, new_ref, out_ref, *, block, old_block):
    head_width = query_ref.shape[1]
    step = pl.program_id(0)
    query_rows = query_ref[...] * jnp.asarray(head_width ** (-0.5), query_ref.dtype)

    def fold(carry, keys, values, mask):
        top, total, weighted = carry
        scores = lax.dot_general(
            query_rows, keys, (((1,), (1,)), ((), ())), preferred_element_type=jnp.float32
        )
        if mask is not None:
            scores = jnp.where(mask, scores, -jnp.inf)
        new_top = jnp.maximum(top, jnp.max(scores, 1, keepdims=True))
        exps = jnp.exp(scores - new_top)
        shrink = jnp.exp(top - new_top)
        total = total * shrink + jnp.sum(exps, 1, keepdims=True)
        weighted = weighted * shrink + jnp.dot(
            exps.astype(jnp.bfloat16), values, preferred_element_type=jnp.float32
        )
        return new_top, total, weighted

    rows = query_rows.shape[0]
    carry = (
        jnp.full((rows, 1), -jnp.inf, jnp.float32),
        jnp.zeros((rows, 1), jnp.float32),
        jnp.zeros((rows, head_width), jnp.float32),
    )
    row_at = lax.broadcasted_iota(jnp.int32, (rows, block), 0)
    col_at = lax.broadcasted_iota(jnp.int32, (rows, block), 1)
    here = pl.ds(step * block, block)
    carry = fold(
        carry, new_ref[here, :head_width], new_ref[here, head_width:], col_at <= row_at
    )
    for old_ref in (cache_ref, other_ref):
        for first in range(0, old_ref.shape[0], old_block):
            part = pl.ds(first, old_block)
            carry = fold(carry, old_ref[part, :head_width], old_ref[part, head_width:], None)

    def earlier(index, carry):
        part = pl.ds(index * block, block)
        return fold(carry, new_ref[part, :head_width], new_ref[part, head_width:], None)

    top, total, weighted = lax.fori_loop(0, step, earlier, carry)
    out_ref[...] = (weighted / total).astype(out_ref.dtype)


def attend(queries, new_pairs, cached, cached_other):
    length, head_width = queries.shape
    block = min(512, length)
    old_block = min(1024, cached.shape[0])
    return pl.pallas_call(
        functools.partial(attend_kernel, block=block, old_block=old_block),
        grid=(length // block,),
        in_specs=[
            pl.BlockSpec((block, head_width), lambda i: (i, 0)),
            pl.BlockSpec(cached.shape, lambda i: (0, 0)),
            pl.BlockSpec(cached_other.shape, lambda i: (0, 0)),
            pl.BlockSpec(new_pairs.shape, lambda i: (0, 0)),
        ],
        out_specs=pl.BlockSpec((block, head_width), lambda i: (i, 0)),
        out_shape=jax.ShapeDtypeStruct((length, head_width), jnp.bfloat16),
        cost_estimate=pl.CostEstimate(
            flops=4 * length * head_width * (length // 2 + 2 * cached.shape[0]),
            bytes_accessed=8 * length * head_width * 2,
            transcendentals=length * (length // 2 + 2 * cached.shape[0]),
        ),
    )(queries, cached, cached_other, new_pairs)


def local(queries, new_kv, cache, resid, w_out, norm_gain, expert_ids, expert_gates, w_in, w_down):
    axis_count = lax.axis_size("head")
    local_rows = queries.shape[0]
    seq_count = queries.shape[1]
    head_count = queries.shape[2]
    head_width = queries.shape[3]
    pair_heads = new_kv.shape[2]
    group_size = head_count // pair_heads
    model_width = resid.shape[2]
    row_count = local_rows * seq_count
    slots = seq_count * pair_heads
    across = [[c * group_size + j for c in range(slots)] for j in range(group_size)]
    inside = [
        [c * group_size + j for j in range(core, group_size, 2)]
        for c in range(slots)
        for core in range(2)
    ]
    parity = lax.axis_index("head") % 2
    query_slots = queries.reshape(local_rows, axis_count, head_width).transpose(1, 0, 2)
    pair_slots = new_kv.reshape(local_rows, slots, 2 * head_width).transpose(1, 0, 2)
    pair_slots = lax.all_to_all(
        pair_slots, "head", split_axis=0, concat_axis=0, axis_index_groups=across, tiled=True
    )
    cache_rows = lax.all_gather(cache[0], "head", axis=0, axis_index_groups=inside, tiled=True)
    head_queries = lax.all_to_all(query_slots, "head", split_axis=0, concat_axis=0, tiled=True)
    same_core = [list(range(core, axis_count, 2)) for core in range(2)]
    half = model_width // 2
    own_half = lax.dynamic_slice_in_dim(w_out, parity * half, half, 2)
    other_half = swap_in_pair(lax.dynamic_slice_in_dim(w_out, (1 - parity) * half, half, 2))
    w_pair = jnp.concatenate(
        [
            jnp.where(parity == 0, own_half, other_half),
            jnp.where(parity == 0, other_half, own_half),
        ],
        1,
    )
    pair_slots, head_queries, cache_rows = lax.optimization_barrier(
        (pair_slots, head_queries, cache_rows)
    )
    pairs = lax.all_gather(pair_slots, "head", axis=0, axis_index_groups=inside, tiled=False)
    cache_other = swap_in_pair(cache_rows)
    pairs, w_pair = lax.optimization_barrier((pairs, w_pair))
    w_half = lax.all_gather(w_pair, "head", axis=1, axis_index_groups=same_core, tiled=True)
    w_half = w_half.reshape(head_count * head_width, half)
    pairs_other = swap_in_pair(pairs)
    pairs = jnp.stack(
        [
            jnp.where(parity == 0, pairs, pairs_other),
            jnp.where(parity == 0, pairs_other, pairs),
        ],
        1,
    )
    pairs = pairs.transpose(2, 0, 1, 3, 4).reshape(axis_count * local_rows, 2 * head_width)
    attended = attend(head_queries.reshape(-1, head_width), pairs, cache_rows, cache_other)
    returned = lax.all_to_all(
        attended.reshape(axis_count, local_rows, head_width),
        "head",
        split_axis=0,
        concat_axis=0,
        tiled=True,
    )
    attn_rows = returned.reshape(seq_count, head_count, local_rows, head_width)
    attn_rows = attn_rows.transpose(2, 0, 1, 3).reshape(row_count, head_count * head_width)
    partner_rows = swap_in_pair(attn_rows)
    partner_part = jnp.dot(partner_rows, w_half, preferred_element_type=jnp.float32)
    far_part = swap_in_pair(partner_part)
    near_part = jnp.dot(attn_rows, w_half, preferred_element_type=jnp.float32)
    projected = jnp.concatenate(
        [
            jnp.where(parity == 0, near_part, far_part),
            jnp.where(parity == 0, far_part, near_part),
        ],
        1,
    )
    stream = resid.reshape(row_count, model_width).astype(jnp.float32) + projected
    normed = stream * lax.rsqrt(jnp.mean(stream * stream, 1, keepdims=True) + eps_norm) * norm_gain
    normed = normed.astype(jnp.bfloat16)
    top_count = expert_ids.shape[2]
    flat_ids = expert_ids.reshape(-1)
    local_experts = w_in.shape[0]
    experts = local_experts * axis_count
    capacity = max(2, 2 * row_count * top_count // experts)
    onehot = (flat_ids[:, None] == jnp.arange(experts, dtype=jnp.int32)[None, :]).astype(jnp.int32)
    earlier = jnp.cumsum(onehot, 0) - onehot
    slot_rank = jnp.sum(earlier * onehot, 1)
    target = flat_ids * capacity + slot_rank
    target = target.reshape(row_count, top_count)
    places = jnp.arange(experts * capacity, dtype=jnp.int32)
    chosen = jnp.zeros((experts * capacity, row_count), jnp.bool_)
    gate_of = jnp.zeros((row_count, experts * capacity), jnp.float32)
    gates = expert_gates.reshape(row_count, top_count)
    for rank in range(top_count):
        chosen = chosen | (places[:, None] == target[None, :, rank])
        gate_of = jnp.where(
            target[:, rank, None] == places[None, :], gates[:, rank, None], gate_of
        )
    outgoing = jnp.dot(
        chosen.astype(jnp.bfloat16), normed, preferred_element_type=jnp.float32
    ).astype(jnp.bfloat16)
    outgoing = outgoing.reshape(axis_count, local_experts, capacity, model_width)
    hidden_width = w_down.shape[1]
    inner_act = jnp.einsum(
        "semd,edf->semf",
        lax.all_to_all(outgoing, "head", split_axis=0, concat_axis=0, tiled=True),
        w_in,
        preferred_element_type=jnp.float32,
    )
    hidden = (jax.nn.silu(inner_act[..., :hidden_width]) * inner_act[..., hidden_width:]).astype(
        jnp.bfloat16
    )
    answered = jnp.einsum(
        "semf,efd->semd", hidden, w_down, preferred_element_type=jnp.float32
    ).astype(jnp.bfloat16)
    returned_rows = lax.all_to_all(answered, "head", split_axis=0, concat_axis=0, tiled=True)
    picked = returned_rows.reshape(experts * capacity, model_width)
    expert_sum = jnp.zeros((row_count, model_width), jnp.float32)
    rest = gate_of
    for _ in range(3):
        term = lax.reduce_precision(rest, 8, 7)
        rest = rest - term
        expert_sum = expert_sum + jnp.dot(
            term.astype(jnp.bfloat16), picked, preferred_element_type=jnp.float32
        )
    return (stream + expert_sum).astype(jnp.bfloat16).reshape(local_rows, seq_count, model_width)


def solution(mesh):
    return jax.shard_map(
        local,
        mesh=mesh,
        in_specs=(
            P("head", "grp", None, None),
            P("head", "grp", None, None),
            P(("grp", "head"), None, None),
            P("head", "grp", None),
            P(None, "head", None),
            P(),
            P("head", "grp", None),
            P("head", "grp", None),
            P("head", None, None),
            P("head", None, None),
        ),
        out_specs=P("head", "grp", None),
        check_vma=False,
    )
```

```python
import functools

import jax
import jax.numpy as jnp
from jax import lax
from jax.experimental import pallas as pl
from jax.experimental.pallas import tpu as pltpu
from jax.sharding import PartitionSpec as P

eps_norm = 1e-06


def partner_2(value, stride):
    mask = 2**stride
    pairs = [(source, source ^ mask) for source in range(lax.axis_size("head"))]
    return lax.ppermute(value, "head", pairs)


def turn_grp(value, shift):
    count = lax.axis_size("grp")
    return lax.ppermute(value, "grp", [(i, (i + shift) % count) for i in range(count)])


def attend_kernel(
    me_ref, query_ref, cache_ref, other_ref, pairs_ref, out_ref, new_ref, *, block, old_block, order
):
    head_width = query_ref.shape[1]
    step = pl.program_id(0)
    members, slots, local_rows = pairs_ref.shape[:3]

    @pl.when(step == 0)
    def _():
        for slot in range(slots):
            for member in range(members):
                apart = member ^ me_ref[0]
                place = 0
                for rank, bit in enumerate(order):
                    place = place + ((apart >> bit) & 1) * 2**rank
                first = (slot * members + member) * local_rows
                new_ref[first : first + local_rows, :] = pairs_ref[place, slot]

    query_rows = query_ref[...] * jnp.asarray(head_width ** (-0.5), query_ref.dtype)

    def fold(carry, keys, values, mask):
        top, total, weighted = carry
        scores = lax.dot_general(
            query_rows, keys, (((1,), (1,)), ((), ())), preferred_element_type=jnp.float32
        )
        if mask is not None:
            scores = jnp.where(mask, scores, -jnp.inf)
        new_top = jnp.maximum(top, jnp.max(scores, 1, keepdims=True))
        exps = jnp.exp(scores - new_top)
        shrink = jnp.exp(top - new_top)
        total = total * shrink + jnp.sum(exps, 1, keepdims=True)
        weighted = weighted * shrink + jnp.dot(
            exps.astype(jnp.bfloat16), values, preferred_element_type=jnp.float32
        )
        return new_top, total, weighted

    rows = query_rows.shape[0]
    carry = (
        jnp.full((rows, 1), -jnp.inf, jnp.float32),
        jnp.zeros((rows, 1), jnp.float32),
        jnp.zeros((rows, head_width), jnp.float32),
    )
    row_at = lax.broadcasted_iota(jnp.int32, (rows, block), 0)
    col_at = lax.broadcasted_iota(jnp.int32, (rows, block), 1)
    here = pl.ds(step * block, block)
    carry = fold(
        carry, new_ref[here, :head_width], new_ref[here, head_width:], col_at <= row_at
    )
    for old_ref in (cache_ref, other_ref):
        for first in range(0, old_ref.shape[0], old_block):
            part = pl.ds(first, old_block)
            carry = fold(carry, old_ref[part, :head_width], old_ref[part, head_width:], None)

    def earlier(index, carry):
        part = pl.ds(index * block, block)
        return fold(carry, new_ref[part, :head_width], new_ref[part, head_width:], None)

    top, total, weighted = lax.fori_loop(0, step, earlier, carry)
    out_ref[...] = (weighted / total).astype(out_ref.dtype)


def attend(me, queries, new_pairs, cached, cached_other, order):
    length, head_width = queries.shape
    block = min(512, length)
    old_block = min(1024, cached.shape[0])
    return pl.pallas_call(
        functools.partial(attend_kernel, block=block, old_block=old_block, order=order),
        grid_spec=pltpu.PrefetchScalarGridSpec(
            num_scalar_prefetch=1,
            grid=(length // block,),
            in_specs=[
                pl.BlockSpec((block, head_width), lambda i, me: (i, 0)),
                pl.BlockSpec(cached.shape, lambda i, me: (0, 0)),
                pl.BlockSpec(cached_other.shape, lambda i, me: (0, 0)),
                pl.BlockSpec(new_pairs.shape, lambda i, me: (0, 0, 0, 0)),
            ],
            out_specs=pl.BlockSpec((block, head_width), lambda i, me: (i, 0)),
            scratch_shapes=[pltpu.VMEM((length, 2 * head_width), jnp.bfloat16)],
        ),
        out_shape=jax.ShapeDtypeStruct((length, head_width), jnp.bfloat16),
        cost_estimate=pl.CostEstimate(
            flops=4 * length * head_width * (length // 2 + 2 * cached.shape[0]),
            bytes_accessed=8 * length * head_width * 2,
            transcendentals=length * (length // 2 + 2 * cached.shape[0]),
        ),
    )(me, queries, cached, cached_other, new_pairs)


def local(queries, new_kv, cache, resid, w_out, norm_gain, expert_ids, expert_gates, w_in, w_down):
    axis_count = lax.axis_size("head")
    local_rows = queries.shape[0]
    seq_count = queries.shape[1]
    head_count = queries.shape[2]
    head_width = queries.shape[3]
    pair_heads = new_kv.shape[2]
    group_size = head_count // pair_heads
    model_width = resid.shape[2]
    row_count = local_rows * seq_count
    slots = seq_count * pair_heads
    across = [[c * group_size + j for c in range(slots)] for j in range(group_size)]
    query_slots = queries.reshape(local_rows, axis_count, head_width).transpose(1, 0, 2)
    pair_slots = new_kv.reshape(local_rows, slots, 2 * head_width).transpose(1, 0, 2)
    pair_slots = lax.all_to_all(
        pair_slots, "head", split_axis=0, concat_axis=0, axis_index_groups=across, tiled=True
    )
    grp_count = lax.axis_size("grp")
    grp_me = lax.axis_index("grp")
    part_width = model_width // grp_count
    w_part = lax.dynamic_slice_in_dim(w_out, grp_me * part_width, part_width, 2)
    w_part = lax.all_gather(w_part, "head", axis=1, tiled=True)
    w_part = w_part.reshape(head_count * head_width, part_width)
    bits = group_size.bit_length() - 1
    order = tuple(range(1, bits)) + (0,)
    cache_rows = cache[0]
    pairs = pair_slots[None]
    for bit in order[:-1]:
        cache_rows = jnp.concatenate([cache_rows, partner_2(cache_rows, bit)], 0)
    cache_other = partner_2(cache_rows, 0)
    head_queries = lax.all_to_all(query_slots, "head", split_axis=0, concat_axis=0, tiled=True)
    for bit in order:
        pairs = jnp.concatenate([pairs, partner_2(pairs, bit)], 0)
    me = (lax.axis_index("head") % group_size).astype(jnp.int32).reshape(1)
    attended = attend(
        me, head_queries.reshape(-1, head_width), pairs, cache_rows, cache_other, order
    )
    returned = lax.all_to_all(
        attended.reshape(axis_count, local_rows, head_width),
        "head",
        split_axis=0,
        concat_axis=0,
        tiled=True,
    )
    attn_rows = returned.reshape(seq_count, head_count, local_rows, head_width)
    attn_rows = attn_rows.transpose(2, 0, 1, 3).reshape(row_count, head_count * head_width)
    parts = []
    for shift in range(1, grp_count):
        far_rows = turn_grp(attn_rows, shift)
        far_part = jnp.dot(far_rows, w_part, preferred_element_type=jnp.float32)
        parts.append(turn_grp(far_part, -shift))
    projected = []
    near_part = jnp.dot(attn_rows, w_part, preferred_element_type=jnp.float32)
    for column in range(grp_count):
        piece = near_part
        for shift in range(1, grp_count):
            piece = jnp.where((grp_me + shift) % grp_count == column, parts[shift - 1], piece)
        projected.append(piece)
    projected = jnp.concatenate(projected, 1)
    stream = resid.reshape(row_count, model_width).astype(jnp.float32) + projected
    normed = stream * lax.rsqrt(jnp.mean(stream * stream, 1, keepdims=True) + eps_norm) * norm_gain
    normed = normed.astype(jnp.bfloat16)
    top_count = expert_ids.shape[2]
    flat_ids = expert_ids.reshape(-1)
    local_experts = w_in.shape[0]
    experts = local_experts * axis_count
    capacity = max(2, 2 * row_count * top_count // experts)
    onehot = (flat_ids[:, None] == jnp.arange(experts, dtype=jnp.int32)[None, :]).astype(jnp.int32)
    earlier = jnp.cumsum(onehot, 0) - onehot
    slot_rank = jnp.sum(earlier * onehot, 1)
    target = flat_ids * capacity + slot_rank
    target = target.reshape(row_count, top_count)
    places = jnp.arange(experts * capacity, dtype=jnp.int32)
    chosen = jnp.zeros((experts * capacity, row_count), jnp.bool_)
    gate_of = jnp.zeros((row_count, experts * capacity), jnp.float32)
    gates = expert_gates.reshape(row_count, top_count)
    for rank in range(top_count):
        chosen = chosen | (places[:, None] == target[None, :, rank])
        gate_of = jnp.where(
            target[:, rank, None] == places[None, :], gates[:, rank, None], gate_of
        )
    outgoing = jnp.dot(
        chosen.astype(jnp.bfloat16), normed, preferred_element_type=jnp.float32
    ).astype(jnp.bfloat16)
    outgoing = outgoing.reshape(axis_count, local_experts, capacity, model_width)
    hidden_width = w_down.shape[1]
    inner_act = jnp.einsum(
        "semd,edf->semf",
        lax.all_to_all(outgoing, "head", split_axis=0, concat_axis=0, tiled=True),
        w_in,
        preferred_element_type=jnp.float32,
    )
    hidden = (jax.nn.silu(inner_act[..., :hidden_width]) * inner_act[..., hidden_width:]).astype(
        jnp.bfloat16
    )
    answered = jnp.einsum(
        "semf,efd->semd", hidden, w_down, preferred_element_type=jnp.float32
    ).astype(jnp.bfloat16)
    returned_rows = lax.all_to_all(answered, "head", split_axis=0, concat_axis=0, tiled=True)
    picked = returned_rows.reshape(experts * capacity, model_width)
    expert_sum = jnp.zeros((row_count, model_width), jnp.float32)
    rest = gate_of
    for _ in range(3):
        term = lax.reduce_precision(rest, 8, 7)
        rest = rest - term
        expert_sum = expert_sum + jnp.dot(
            term.astype(jnp.bfloat16), picked, preferred_element_type=jnp.float32
        )
    return (stream + expert_sum).astype(jnp.bfloat16).reshape(local_rows, seq_count, model_width)


def solution(mesh):
    return jax.shard_map(
        local,
        mesh=mesh,
        in_specs=(
            P("head", "grp", None, None),
            P("head", "grp", None, None),
            P(("grp", "head"), None, None),
            P("head", "grp", None),
            P(None, "head", None),
            P(),
            P("head", "grp", None),
            P("head", "grp", None),
            P("head", None, None),
            P("head", None, None),
        ),
        out_specs=P("head", "grp", None),
        check_vma=False,
    )
```

```python
import functools

import jax
import jax.numpy as jnp
from jax import lax
from jax.experimental import pallas as pl
from jax.experimental.pallas import tpu as pltpu
from jax.sharding import PartitionSpec as P

eps_norm = 1e-06


def partner_2(value, stride):
    mask = 2**stride
    pairs = [(source, source ^ mask) for source in range(lax.axis_size("head"))]
    return lax.ppermute(value, "head", pairs)


def turn_grp(value, shift):
    count = lax.axis_size("grp")
    return lax.ppermute(value, "grp", [(i, (i + shift) % count) for i in range(count)])


def attend_kernel(
    me_ref, query_ref, cache_ref, other_ref, pairs_ref, out_ref, new_ref, *, block, old_block, order
):
    head_width = query_ref.shape[1]
    step = pl.program_id(0)
    members, slots, local_rows = pairs_ref.shape[:3]

    @pl.when(step == 0)
    def _():
        for slot in range(slots):
            for member in range(members):
                apart = member ^ me_ref[0]
                place = 0
                for rank, bit in enumerate(order):
                    place = place + ((apart >> bit) & 1) * 2**rank
                first = (slot * members + member) * local_rows
                new_ref[first : first + local_rows, :] = pairs_ref[place, slot]

    query_rows = query_ref[...] * jnp.asarray(head_width ** (-0.5), query_ref.dtype)

    def fold(carry, keys, values, mask):
        top, total, weighted = carry
        scores = lax.dot_general(
            query_rows, keys, (((1,), (1,)), ((), ())), preferred_element_type=jnp.float32
        )
        if mask is not None:
            scores = jnp.where(mask, scores, -jnp.inf)
        new_top = jnp.maximum(top, jnp.max(scores, 1, keepdims=True))
        exps = jnp.exp(scores - new_top)
        shrink = jnp.exp(top - new_top)
        total = total * shrink + jnp.sum(exps, 1, keepdims=True)
        weighted = weighted * shrink + jnp.dot(
            exps.astype(jnp.bfloat16), values, preferred_element_type=jnp.float32
        )
        return new_top, total, weighted

    rows = query_rows.shape[0]
    carry = (
        jnp.full((rows, 1), -jnp.inf, jnp.float32),
        jnp.zeros((rows, 1), jnp.float32),
        jnp.zeros((rows, head_width), jnp.float32),
    )
    row_at = lax.broadcasted_iota(jnp.int32, (rows, block), 0)
    col_at = lax.broadcasted_iota(jnp.int32, (rows, block), 1)
    here = pl.ds(step * block, block)
    carry = fold(
        carry, new_ref[here, :head_width], new_ref[here, head_width:], col_at <= row_at
    )
    for old_ref in (cache_ref, other_ref):
        for first in range(0, old_ref.shape[0], old_block):
            part = pl.ds(first, old_block)
            carry = fold(carry, old_ref[part, :head_width], old_ref[part, head_width:], None)

    def earlier(index, carry):
        part = pl.ds(index * block, block)
        return fold(carry, new_ref[part, :head_width], new_ref[part, head_width:], None)

    top, total, weighted = lax.fori_loop(0, step, earlier, carry)
    out_ref[...] = (weighted / total).astype(out_ref.dtype)


def attend(me, queries, new_pairs, cached, cached_other, order):
    length, head_width = queries.shape
    block = min(512, length)
    old_block = min(1024, cached.shape[0])
    return pl.pallas_call(
        functools.partial(attend_kernel, block=block, old_block=old_block, order=order),
        grid_spec=pltpu.PrefetchScalarGridSpec(
            num_scalar_prefetch=1,
            grid=(length // block,),
            in_specs=[
                pl.BlockSpec((block, head_width), lambda i, me: (i, 0)),
                pl.BlockSpec(cached.shape, lambda i, me: (0, 0)),
                pl.BlockSpec(cached_other.shape, lambda i, me: (0, 0)),
                pl.BlockSpec(new_pairs.shape, lambda i, me: (0, 0, 0, 0)),
            ],
            out_specs=pl.BlockSpec((block, head_width), lambda i, me: (i, 0)),
            scratch_shapes=[pltpu.VMEM((length, 2 * head_width), jnp.bfloat16)],
        ),
        out_shape=jax.ShapeDtypeStruct((length, head_width), jnp.bfloat16),
        cost_estimate=pl.CostEstimate(
            flops=4 * length * head_width * (length // 2 + 2 * cached.shape[0]),
            bytes_accessed=8 * length * head_width * 2,
            transcendentals=length * (length // 2 + 2 * cached.shape[0]),
        ),
    )(me, queries, cached, cached_other, new_pairs)


def local(queries, new_kv, cache, resid, w_out, norm_gain, expert_ids, expert_gates, w_in, w_down):
    axis_count = lax.axis_size("head")
    local_rows = queries.shape[0]
    seq_count = queries.shape[1]
    head_count = queries.shape[2]
    head_width = queries.shape[3]
    pair_heads = new_kv.shape[2]
    group_size = head_count // pair_heads
    model_width = resid.shape[2]
    row_count = local_rows * seq_count
    slots = seq_count * pair_heads
    across = [[c * group_size + j for c in range(slots)] for j in range(group_size)]
    query_slots = queries.reshape(local_rows, axis_count, head_width).transpose(1, 0, 2)
    pair_slots = new_kv.reshape(local_rows, slots, 2 * head_width).transpose(1, 0, 2)
    pair_slots = lax.all_to_all(
        pair_slots, "head", split_axis=0, concat_axis=0, axis_index_groups=across, tiled=True
    )
    grp_count = lax.axis_size("grp")
    grp_me = lax.axis_index("grp")
    part_width = model_width // grp_count
    w_part = lax.dynamic_slice_in_dim(w_out, grp_me * part_width, part_width, 2)
    bits = group_size.bit_length() - 1
    order = tuple(range(1, bits)) + (0,)
    cache_rows = cache[0]
    pairs = pair_slots[None]
    for bit in order[:-1]:
        cache_rows = jnp.concatenate([cache_rows, partner_2(cache_rows, bit)], 0)
    head_queries = lax.all_to_all(query_slots, "head", split_axis=0, concat_axis=0, tiled=True)
    for bit in order[:-1]:
        pairs = jnp.concatenate([pairs, partner_2(pairs, bit)], 0)
    w_part, pairs, cache_rows, head_queries = lax.optimization_barrier(
        (w_part, pairs, cache_rows, head_queries)
    )
    w_part = lax.all_gather(w_part, "head", axis=1, tiled=True)
    w_part = w_part.reshape(head_count * head_width, part_width)
    cache_other = partner_2(cache_rows, 0)
    pairs = jnp.concatenate([pairs, partner_2(pairs, 0)], 0)
    me = (lax.axis_index("head") % group_size).astype(jnp.int32).reshape(1)
    attended = attend(
        me, head_queries.reshape(-1, head_width), pairs, cache_rows, cache_other, order
    )
    returned = lax.all_to_all(
        attended.reshape(axis_count, local_rows, head_width),
        "head",
        split_axis=0,
        concat_axis=0,
        tiled=True,
    )
    attn_rows = returned.reshape(seq_count, head_count, local_rows, head_width)
    attn_rows = attn_rows.transpose(2, 0, 1, 3).reshape(row_count, head_count * head_width)
    parts = []
    for shift in range(1, grp_count):
        far_rows = turn_grp(attn_rows, shift)
        far_part = jnp.dot(far_rows, w_part, preferred_element_type=jnp.float32)
        parts.append(turn_grp(far_part.astype(jnp.bfloat16), -shift).astype(jnp.float32))
    projected = []
    near_part = jnp.dot(attn_rows, w_part, preferred_element_type=jnp.float32)
    for column in range(grp_count):
        piece = near_part
        for shift in range(1, grp_count):
            piece = jnp.where((grp_me + shift) % grp_count == column, parts[shift - 1], piece)
        projected.append(piece)
    projected = jnp.concatenate(projected, 1)
    stream = resid.reshape(row_count, model_width).astype(jnp.float32) + projected
    normed = stream * lax.rsqrt(jnp.mean(stream * stream, 1, keepdims=True) + eps_norm) * norm_gain
    normed = normed.astype(jnp.bfloat16)
    top_count = expert_ids.shape[2]
    flat_ids = expert_ids.reshape(-1)
    local_experts = w_in.shape[0]
    experts = local_experts * axis_count
    capacity = max(2, 2 * row_count * top_count // experts)
    onehot = (flat_ids[:, None] == jnp.arange(experts, dtype=jnp.int32)[None, :]).astype(jnp.int32)
    earlier = jnp.cumsum(onehot, 0) - onehot
    slot_rank = jnp.sum(earlier * onehot, 1)
    target = flat_ids * capacity + slot_rank
    target = target.reshape(row_count, top_count)
    places = jnp.arange(experts * capacity, dtype=jnp.int32)
    chosen = jnp.zeros((experts * capacity, row_count), jnp.bool_)
    gate_of = jnp.zeros((row_count, experts * capacity), jnp.float32)
    gates = expert_gates.reshape(row_count, top_count)
    for rank in range(top_count):
        chosen = chosen | (places[:, None] == target[None, :, rank])
        gate_of = jnp.where(
            target[:, rank, None] == places[None, :], gates[:, rank, None], gate_of
        )
    outgoing = jnp.dot(
        chosen.astype(jnp.bfloat16), normed, preferred_element_type=jnp.float32
    ).astype(jnp.bfloat16)
    outgoing = outgoing.reshape(axis_count, local_experts, capacity, model_width)
    hidden_width = w_down.shape[1]
    inner_act = jnp.einsum(
        "semd,edf->semf",
        lax.all_to_all(outgoing, "head", split_axis=0, concat_axis=0, tiled=True),
        w_in,
        preferred_element_type=jnp.float32,
    )
    hidden = (jax.nn.silu(inner_act[..., :hidden_width]) * inner_act[..., hidden_width:]).astype(
        jnp.bfloat16
    )
    answered = jnp.einsum(
        "semf,efd->semd", hidden, w_down, preferred_element_type=jnp.float32
    ).astype(jnp.bfloat16)
    returned_rows = lax.all_to_all(answered, "head", split_axis=0, concat_axis=0, tiled=True)
    picked = returned_rows.reshape(experts * capacity, model_width)
    expert_sum = jnp.zeros((row_count, model_width), jnp.float32)
    rest = gate_of
    for _ in range(3):
        term = lax.reduce_precision(rest, 8, 7)
        rest = rest - term
        expert_sum = expert_sum + jnp.dot(
            term.astype(jnp.bfloat16), picked, preferred_element_type=jnp.float32
        )
    return (stream + expert_sum).astype(jnp.bfloat16).reshape(local_rows, seq_count, model_width)


def solution(mesh):
    return jax.shard_map(
        local,
        mesh=mesh,
        in_specs=(
            P("head", "grp", None, None),
            P("head", "grp", None, None),
            P(("grp", "head"), None, None),
            P("head", "grp", None),
            P(None, "head", None),
            P(),
            P("head", "grp", None),
            P("head", "grp", None),
            P("head", None, None),
            P("head", None, None),
        ),
        out_specs=P("head", "grp", None),
        check_vma=False,
    )
```

```python
import functools

import jax
import jax.numpy as jnp
from jax import lax
from jax.experimental import pallas as pl
from jax.experimental.pallas import tpu as pltpu
from jax.sharding import PartitionSpec as P

eps_norm = 1e-06


def partner_2(value, stride):
    mask = 2**stride
    pairs = [(source, source ^ mask) for source in range(lax.axis_size("head"))]
    return lax.ppermute(value, "head", pairs)


def turn_grp(value, shift):
    count = lax.axis_size("grp")
    return lax.ppermute(value, "grp", [(i, (i + shift) % count) for i in range(count)])


def attend_kernel(
    me_ref, query_ref, cache_ref, other_ref, pairs_ref, out_ref, new_ref, *, block, old_block, order
):
    head_width = query_ref.shape[1]
    step = pl.program_id(0)
    members, slots, local_rows = pairs_ref.shape[:3]

    @pl.when(step == 0)
    def _():
        for slot in range(slots):
            for member in range(members):
                apart = member ^ me_ref[0]
                place = 0
                for rank, bit in enumerate(order):
                    place = place + ((apart >> bit) & 1) * 2**rank
                first = (slot * members + member) * local_rows
                new_ref[first : first + local_rows, :] = pairs_ref[place, slot]

    query_rows = query_ref[...] * jnp.asarray(head_width ** (-0.5), query_ref.dtype)

    def fold(carry, keys, values, mask):
        top, total, weighted = carry
        scores = lax.dot_general(
            query_rows, keys, (((1,), (1,)), ((), ())), preferred_element_type=jnp.float32
        )
        if mask is not None:
            scores = jnp.where(mask, scores, -jnp.inf)
        new_top = jnp.maximum(top, jnp.max(scores, 1, keepdims=True))
        exps = jnp.exp(scores - new_top)
        shrink = jnp.exp(top - new_top)
        total = total * shrink + jnp.sum(exps, 1, keepdims=True)
        weighted = weighted * shrink + jnp.dot(
            exps.astype(jnp.bfloat16), values, preferred_element_type=jnp.float32
        )
        return new_top, total, weighted

    rows = query_rows.shape[0]
    carry = (
        jnp.full((rows, 1), -jnp.inf, jnp.float32),
        jnp.zeros((rows, 1), jnp.float32),
        jnp.zeros((rows, head_width), jnp.float32),
    )
    row_at = lax.broadcasted_iota(jnp.int32, (rows, block), 0)
    col_at = lax.broadcasted_iota(jnp.int32, (rows, block), 1)
    here = pl.ds(step * block, block)
    carry = fold(
        carry, new_ref[here, :head_width], new_ref[here, head_width:], col_at <= row_at
    )
    for old_ref in (cache_ref, other_ref):
        for first in range(0, old_ref.shape[0], old_block):
            part = pl.ds(first, old_block)
            carry = fold(carry, old_ref[part, :head_width], old_ref[part, head_width:], None)

    def earlier(index, carry):
        part = pl.ds(index * block, block)
        return fold(carry, new_ref[part, :head_width], new_ref[part, head_width:], None)

    top, total, weighted = lax.fori_loop(0, step, earlier, carry)
    out_ref[...] = (weighted / total).astype(out_ref.dtype)


def attend(me, queries, new_pairs, cached, cached_other, order):
    length, head_width = queries.shape
    block = min(512, length)
    old_block = min(1024, cached.shape[0])
    return pl.pallas_call(
        functools.partial(attend_kernel, block=block, old_block=old_block, order=order),
        grid_spec=pltpu.PrefetchScalarGridSpec(
            num_scalar_prefetch=1,
            grid=(length // block,),
            in_specs=[
                pl.BlockSpec((block, head_width), lambda i, me: (i, 0)),
                pl.BlockSpec(cached.shape, lambda i, me: (0, 0)),
                pl.BlockSpec(cached_other.shape, lambda i, me: (0, 0)),
                pl.BlockSpec(new_pairs.shape, lambda i, me: (0, 0, 0, 0)),
            ],
            out_specs=pl.BlockSpec((block, head_width), lambda i, me: (i, 0)),
            scratch_shapes=[pltpu.VMEM((length, 2 * head_width), jnp.bfloat16)],
        ),
        out_shape=jax.ShapeDtypeStruct((length, head_width), jnp.bfloat16),
        cost_estimate=pl.CostEstimate(
            flops=4 * length * head_width * (length // 2 + 2 * cached.shape[0]),
            bytes_accessed=8 * length * head_width * 2,
            transcendentals=length * (length // 2 + 2 * cached.shape[0]),
        ),
    )(me, queries, cached, cached_other, new_pairs)


def local(queries, new_kv, cache, resid, w_out, norm_gain, expert_ids, expert_gates, w_in, w_down):
    axis_count = lax.axis_size("head")
    local_rows = queries.shape[0]
    seq_count = queries.shape[1]
    head_count = queries.shape[2]
    head_width = queries.shape[3]
    pair_heads = new_kv.shape[2]
    group_size = head_count // pair_heads
    model_width = resid.shape[2]
    row_count = local_rows * seq_count
    slots = seq_count * pair_heads
    across = [[c * group_size + j for c in range(slots)] for j in range(group_size)]
    query_slots = queries.reshape(local_rows, axis_count, head_width).transpose(1, 0, 2)
    pair_slots = new_kv.reshape(local_rows, slots, 2 * head_width).transpose(1, 0, 2)
    pair_slots = lax.all_to_all(
        pair_slots, "head", split_axis=0, concat_axis=0, axis_index_groups=across, tiled=True
    )
    grp_count = lax.axis_size("grp")
    grp_me = lax.axis_index("grp")
    part_width = model_width // grp_count
    w_part = lax.dynamic_slice_in_dim(w_out, grp_me * part_width, part_width, 2)
    bits = group_size.bit_length() - 1
    order = tuple(range(1, bits)) + (0,)
    cache_rows = cache[0]
    pairs = pair_slots[None]
    for bit in order[:-1]:
        cache_rows = jnp.concatenate([cache_rows, partner_2(cache_rows, bit)], 0)
    head_queries = lax.all_to_all(query_slots, "head", split_axis=0, concat_axis=0, tiled=True)
    for bit in order[:-1]:
        pairs = jnp.concatenate([pairs, partner_2(pairs, bit)], 0)
    w_part, pairs, cache_rows = lax.optimization_barrier((w_part, pairs, cache_rows))
    w_part = lax.all_gather(w_part, "head", axis=1, tiled=True)
    w_part = w_part.reshape(head_count * head_width, part_width)
    cache_other = partner_2(cache_rows, 0)
    pairs = jnp.concatenate([pairs, partner_2(pairs, 0)], 0)
    me = (lax.axis_index("head") % group_size).astype(jnp.int32).reshape(1)
    attended = attend(
        me, head_queries.reshape(-1, head_width), pairs, cache_rows, cache_other, order
    )
    returned = lax.all_to_all(
        attended.reshape(axis_count, local_rows, head_width),
        "head",
        split_axis=0,
        concat_axis=0,
        tiled=True,
    )
    attn_rows = returned.reshape(seq_count, head_count, local_rows, head_width)
    attn_rows = attn_rows.transpose(2, 0, 1, 3).reshape(row_count, head_count * head_width)
    parts = []
    for shift in range(1, grp_count):
        far_rows = turn_grp(attn_rows, shift)
        far_part = jnp.dot(far_rows, w_part, preferred_element_type=jnp.float32)
        parts.append(turn_grp(far_part.astype(jnp.bfloat16), -shift).astype(jnp.float32))
    projected = []
    near_part = jnp.dot(attn_rows, w_part, preferred_element_type=jnp.float32)
    for column in range(grp_count):
        piece = near_part
        for shift in range(1, grp_count):
            piece = jnp.where((grp_me + shift) % grp_count == column, parts[shift - 1], piece)
        projected.append(piece)
    projected = jnp.concatenate(projected, 1)
    stream = resid.reshape(row_count, model_width).astype(jnp.float32) + projected
    normed = stream * lax.rsqrt(jnp.mean(stream * stream, 1, keepdims=True) + eps_norm) * norm_gain
    normed = normed.astype(jnp.bfloat16)
    top_count = expert_ids.shape[2]
    flat_ids = expert_ids.reshape(-1)
    local_experts = w_in.shape[0]
    experts = local_experts * axis_count
    capacity = max(2, 2 * row_count * top_count // experts)
    onehot = (flat_ids[:, None] == jnp.arange(experts, dtype=jnp.int32)[None, :]).astype(jnp.int32)
    earlier = jnp.cumsum(onehot, 0) - onehot
    slot_rank = jnp.sum(earlier * onehot, 1)
    target = flat_ids * capacity + slot_rank
    target = target.reshape(row_count, top_count)
    places = jnp.arange(experts * capacity, dtype=jnp.int32)
    chosen = jnp.zeros((experts * capacity, row_count), jnp.bool_)
    gate_of = jnp.zeros((row_count, experts * capacity), jnp.float32)
    gates = expert_gates.reshape(row_count, top_count)
    for rank in range(top_count):
        chosen = chosen | (places[:, None] == target[None, :, rank])
        gate_of = jnp.where(
            target[:, rank, None] == places[None, :], gates[:, rank, None], gate_of
        )
    outgoing = jnp.dot(
        chosen.astype(jnp.bfloat16), normed, preferred_element_type=jnp.float32
    ).astype(jnp.bfloat16)
    outgoing = outgoing.reshape(axis_count, local_experts, capacity, model_width)
    hidden_width = w_down.shape[1]
    inner_act = jnp.einsum(
        "semd,edf->semf",
        lax.all_to_all(outgoing, "head", split_axis=0, concat_axis=0, tiled=True),
        w_in,
        preferred_element_type=jnp.float32,
    )
    hidden = (jax.nn.silu(inner_act[..., :hidden_width]) * inner_act[..., hidden_width:]).astype(
        jnp.bfloat16
    )
    answered = jnp.einsum(
        "semf,efd->semd", hidden, w_down, preferred_element_type=jnp.float32
    ).astype(jnp.bfloat16)
    returned_rows = lax.all_to_all(answered, "head", split_axis=0, concat_axis=0, tiled=True)
    picked = returned_rows.reshape(experts * capacity, model_width)
    expert_sum = jnp.zeros((row_count, model_width), jnp.float32)
    rest = gate_of
    for _ in range(3):
        term = lax.reduce_precision(rest, 8, 7)
        rest = rest - term
        expert_sum = expert_sum + jnp.dot(
            term.astype(jnp.bfloat16), picked, preferred_element_type=jnp.float32
        )
    return (stream + expert_sum).astype(jnp.bfloat16).reshape(local_rows, seq_count, model_width)


def solution(mesh):
    return jax.shard_map(
        local,
        mesh=mesh,
        in_specs=(
            P("head", "grp", None, None),
            P("head", "grp", None, None),
            P(("grp", "head"), None, None),
            P("head", "grp", None),
            P(None, "head", None),
            P(),
            P("head", "grp", None),
            P("head", "grp", None),
            P("head", None, None),
            P("head", None, None),
        ),
        out_specs=P("head", "grp", None),
        check_vma=False,
    )
```
